32 devices in a mesh: batch: 8 (over z, y), tensor: 2 (over x), section: 2 (over core).
Axes of the slice: x: 2, y: 2, z: 4, core: 2. Of those that a mesh axis runs over, the one named last changes fastest.
Arguments:
- prefill_cache: bfloat16 [2, 32, 2, 4, 256, 128], P('section', ('batch', 'tensor')), may hold values from -5 to 5
- lengths: int32 [32], P('batch'), may hold values from 1 to 256, as said below
- page_table: int32 [32, 1], P('batch'), may hold values from -1 to 3, as said below
- holder: int32 [8, 4], replicated, may hold values from 0 to 7, as said below
- queries: bfloat16 [32, 2, 4, 32, 128], P(('batch', 'section'), None, None, 'tensor'), may hold values from -120 to 120
- new_kv: bfloat16 [32, 2, 4, 2, 4, 128], P(('batch', 'section'), None, None, None, 'tensor'), may hold values from -5 to 5
Outputs:
- attended: bfloat16 [32, 2, 4, 32, 128], P(('batch', 'section'), None, None, 'tensor')
- decode_pool: bfloat16 [2, 32, 2, 4, 256, 128], P('section', 'batch', None, 'tensor')
The draws below stay inside these ranges and needn't reach their ends.
Inputs may be any that keep to these rules, and one draw needn't show every extreme that they name: Request r's prompt has lengths[r] tokens, held in ceil(lengths[r] / 256) pages. `page_table`: row r names in its first ceil(lengths[r] / 256) columns the pool positions (0 to 3) of the request's pages in order, and -1 after; a position is named at most once among the 4 requests of one batch index; some batch index uses all 4 positions. holder[b, q] = b XOR key_q (bitwise exclusive or of the binary digits), where key_0 to key_7 are distinct numbers of 0 to 7; so each column is a permutation of the batch indices and each row names distinct ones.
All inputs are finite; a program needn't handle non-finite values.
Results may differ from the reference program's by a relative error of at most 0.0038.
Values may be sent and summed in bfloat16 or wider, within the bound.
A program may use at most 64 MiB of HBM per device.

```python
import math
import jax
import jax.numpy as jnp
from jax import lax

HEAD = 128
KV_HEADS = 4
GROUP = 8
PAGE = 256
STEPS = 4
REQ_GRP = 4
LAYERS = 2
Q_HEADS = 32
POSITIONS = 4
REQUESTS = 32
MAX_PAGES = 1
N_BATCH = 8


def page_layout(key):
    base = jax.random.fold_in(key, 11)
    subkeys = jax.random.split(base, 6)
    spare = POSITIONS - REQ_GRP
    width = max(spare, 1)
    extra_total = jax.random.randint(subkeys[0], (N_BATCH,), 0, spare + 1)
    full_group = jax.random.randint(subkeys[5], (), 0, N_BATCH)
    full_request = jax.random.randint(jax.random.fold_in(base, 7), (), 0, REQ_GRP)
    group_ids = jnp.arange(N_BATCH, dtype=jnp.int32)
    request_ids = jnp.arange(REQ_GRP, dtype=jnp.int32)
    is_full = group_ids == full_group
    extra_total = jnp.where(is_full, spare, extra_total)
    target = jax.random.randint(subkeys[1], (N_BATCH, width), 0, REQ_GRP)
    target = jnp.where(is_full[:, None], full_request, target)
    active = jnp.arange(width, dtype=jnp.int32)[None, :] < extra_total[:, None]
    chosen = (target[:, :, None] == request_ids[None, None, :]) & active[:, :, None]
    counts = 1 + jnp.sum(chosen.astype(jnp.int32), axis=1)
    last_part = jax.random.randint(subkeys[2], (N_BATCH, REQ_GRP), 1, PAGE + 1)
    longest = is_full[:, None] & (request_ids[None, :] == full_request)
    last_part = jnp.where(longest, PAGE, last_part)
    lengths = (counts - 1) * PAGE + last_part
    ranking = jax.random.randint(subkeys[3], (N_BATCH, POSITIONS), 0, 1 << 20) * POSITIONS + jnp.arange(POSITIONS, dtype=jnp.int32)[None, :]
    order = jnp.argsort(ranking, axis=1).astype(jnp.int32)
    starts = jnp.cumsum(counts, axis=1) - counts
    column = jnp.arange(MAX_PAGES, dtype=jnp.int32)[None, None, :]
    index = jnp.clip(starts[:, :, None] + column, 0, POSITIONS - 1)
    picked = jnp.take_along_axis(jnp.broadcast_to(order[:, None, :], (N_BATCH, REQ_GRP, POSITIONS)), index, axis=2)
    table = jnp.where(column < counts[:, :, None], picked, -1)
    route_keys = jax.random.permutation(subkeys[4], N_BATCH)[:POSITIONS].astype(jnp.int32)
    holder = jnp.bitwise_xor(group_ids[:, None], route_keys[None, :])
    return (lengths.reshape(REQUESTS).astype(jnp.int32), table.reshape(REQUESTS, MAX_PAGES).astype(jnp.int32), holder.astype(jnp.int32))


def decode_inputs(key):
    base = jax.random.fold_in(key, 23)
    key_pairs, key_queries = jax.random.split(base, 2)
    new_kv = jnp.clip(jax.random.normal(key_pairs, (REQUESTS, LAYERS, STEPS, 2, KV_HEADS, HEAD), jnp.float32), -5.0, 5.0)
    shape = (REQUESTS, LAYERS, STEPS, KV_HEADS, GROUP, HEAD)
    queries = jnp.clip(jax.random.normal(key_queries, shape, jnp.float32), -5.0, 5.0)
    return (queries.reshape(REQUESTS, LAYERS, STEPS, KV_HEADS * GROUP, HEAD).astype(jnp.bfloat16), new_kv.astype(jnp.bfloat16))


def draw_lengths(key, part):
    return page_layout(key)[0]


def draw_page_table(key, part):
    return page_layout(key)[1]


def draw_holder(key, part):
    return page_layout(key)[2]


def draw_queries(key, part):
    return decode_inputs(key)[0]


def draw_new_kv(key, part):
    return decode_inputs(key)[1]


def block_scale(own_key, extent, shards, smallest, high):
    def one(dim, shards_of):
        draws = jax.random.uniform(jax.random.fold_in(jax.random.fold_in(own_key, 6), dim), (shards_of,), jnp.float32, smallest / len(shards), high / len(shards))
        return jnp.repeat(jnp.exp(draws), extent[dim] // shards_of).reshape((-1,) + (1,) * (len(extent) - dim - 1))

    level = one(*shards[0])
    for cut in shards[1:]:
        level = level * one(*cut)
    return level


def noise(key, extent, deviation, most, cuts=(), kind=jnp.bfloat16):
    factor_of = block_scale(key, extent, cuts, -0.22, 0.18) if cuts else 1.0
    drawn = jax.random.normal(key, extent, jnp.float32) * deviation * factor_of
    return jnp.minimum(jnp.maximum(drawn, -most), most).astype(kind)


def setup_inputs(seed: int = 0) -> dict:
    key_of = jax.random.split(jax.random.key(seed), 7)
    prefill_cache = noise(key_of[0], (LAYERS, N_BATCH * POSITIONS, 2, KV_HEADS, PAGE, HEAD), 1.0, 5.0, ((0, 2), (1, 16)))
    lengths = draw_lengths(jax.random.fold_in(key_of[6], 71), 0)
    page_table = draw_page_table(jax.random.fold_in(key_of[6], 71), 0)
    holder = draw_holder(jax.random.fold_in(key_of[6], 71), 0)
    queries = draw_queries(jax.random.fold_in(key_of[6], 71), 0)
    new_kv = draw_new_kv(jax.random.fold_in(key_of[6], 71), 0)
    return dict(prefill_cache=prefill_cache, lengths=lengths, page_table=page_table, holder=holder, queries=queries, new_kv=new_kv)


MASKED = -1e+30

def position_table(lengths, page_table):
    table_rows = page_table.reshape(N_BATCH, REQ_GRP, MAX_PAGES)
    slot_ids = jnp.arange(POSITIONS, dtype=jnp.int32)
    page_hits = (table_rows[:, :, :, None] == slot_ids).astype(jnp.int32)
    in_use = lax.optimization_barrier(jnp.sum(page_hits, axis=(1, 2))) > 0
    request_of = lax.optimization_barrier(jnp.sum(page_hits * jnp.arange(REQ_GRP, dtype=jnp.int32)[None, :, None, None], axis=(1, 2)))
    page_of = lax.optimization_barrier(jnp.sum(page_hits * jnp.arange(MAX_PAGES, dtype=jnp.int32)[None, None, :, None], axis=(1, 2)))
    length_of = lax.optimization_barrier(jnp.sum(page_hits * lengths.reshape(N_BATCH, REQ_GRP)[:, :, None, None], axis=(1, 2)))
    live_count = jnp.clip(length_of - page_of * PAGE, 0, PAGE)
    return (in_use, request_of, live_count)

def block_partials(queries_at, key_rows, value_rows, token_mask):
    score_scale = 1.0 / math.sqrt(HEAD)
    scores = jnp.einsum('nigex,ngpx->ngiep', queries_at.astype(jnp.float32), key_rows.astype(jnp.float32)) * score_scale
    page_peak = lax.optimization_barrier(jnp.max(jnp.where(token_mask, scores, MASKED), axis=-1))
    weights = jnp.where(token_mask, jnp.exp(scores - page_peak[..., None]), 0.0).astype(jnp.bfloat16)
    weight_sum = lax.optimization_barrier(jnp.sum(weights.astype(jnp.float32), axis=-1))
    page_output = jnp.einsum('ngiep,ngpx->ngiex', weights.astype(jnp.float32), value_rows.astype(jnp.float32))
    return (page_peak, weight_sum, page_output)

def reference(prefill_cache, lengths, page_table, holder, queries, new_kv):
    in_use, request_of, live_count = position_table(lengths, page_table)
    slot_ids = jnp.arange(POSITIONS, dtype=jnp.int32)
    batch_ids = jnp.broadcast_to(jnp.arange(N_BATCH, dtype=jnp.int32)[:, None], (N_BATCH, POSITIONS))
    sender_of = jnp.zeros((N_BATCH, POSITIONS), jnp.int32).at[holder, slot_ids[None, :]].set(batch_ids)
    page_cache = prefill_cache.reshape(LAYERS, N_BATCH, POSITIONS, 2, KV_HEADS, PAGE, HEAD)
    moved_pages = page_cache[:, sender_of, slot_ids[None, :]]
    keep_mask = in_use[sender_of, slot_ids[None, :]]
    decode_pool = jnp.where(keep_mask[None, :, :, None, None, None, None], moved_pages, jnp.zeros((), prefill_cache.dtype)).reshape(prefill_cache.shape)
    all_queries = queries.reshape(REQUESTS, LAYERS, STEPS, KV_HEADS, GROUP, HEAD)
    token_index = jnp.arange(PAGE, dtype=jnp.int32)
    step_index = jnp.arange(STEPS, dtype=jnp.int32)
    causal = step_index[None, :] <= step_index[:, None]
    layer_outputs = []
    for layer in range(LAYERS):
        layer_cache = page_cache[layer]
        layer_queries = all_queries[:, layer]

        def group_part(items):
            batch_row, use_row, request_row, live_row = items
            group_pages = lax.dynamic_index_in_dim(layer_cache, batch_row, 0, keepdims=False)
            group_queries = lax.dynamic_slice_in_dim(layer_queries, batch_row * REQ_GRP, REQ_GRP, 0)
            slot_queries = jnp.take(group_queries, request_row, axis=0)
            token_mask = token_index[None, None, None, None, :] < live_row[:, None, None, None, None]
            page_peak, weight_sum, page_output = block_partials(slot_queries, group_pages[:, 0], group_pages[:, 1], token_mask)
            mine = (request_row[None, :] == jnp.arange(REQ_GRP, dtype=jnp.int32)[:, None]) & use_row[None, :]
            row_mask = mine[:, :, None, None, None]
            request_peak = lax.optimization_barrier(jnp.max(jnp.where(row_mask, page_peak[None], MASKED), axis=1))
            factor = jnp.where(row_mask, jnp.exp(page_peak[None] - request_peak[:, None]), 0.0)
            numerator = jnp.einsum('rqgie,qgiex->rgiex', factor, page_output, precision=lax.Precision.HIGHEST)
            denominator = lax.optimization_barrier(jnp.sum(factor * weight_sum[None], axis=1))
            return (request_peak, numerator, denominator)
        request_peak, numerator, denominator = lax.map(group_part, (jnp.arange(N_BATCH, dtype=jnp.int32), in_use, request_of, live_count))
        request_peak = request_peak.reshape(REQUESTS, KV_HEADS, STEPS, GROUP)
        numerator = numerator.reshape(REQUESTS, KV_HEADS, STEPS, GROUP, HEAD)
        denominator = denominator.reshape(REQUESTS, KV_HEADS, STEPS, GROUP)
        new_keys = jnp.transpose(new_kv[:, layer, :, 0], (0, 2, 1, 3))
        new_values = jnp.transpose(new_kv[:, layer, :, 1], (0, 2, 1, 3))
        new_peak, new_sum, new_output = block_partials(layer_queries, new_keys, new_values, causal[None, None, :, None, :])
        joint_peak = jnp.maximum(request_peak, new_peak)
        old_scale = jnp.exp(request_peak - joint_peak)
        new_scale = jnp.exp(new_peak - joint_peak)
        result = (old_scale[..., None] * numerator + new_scale[..., None] * new_output) / (old_scale * denominator + new_scale * new_sum)[..., None]
        layer_outputs.append(jnp.transpose(result, (0, 2, 1, 3, 4)).reshape(REQUESTS, STEPS, Q_HEADS, HEAD))
    attended = jnp.stack(layer_outputs, axis=1).astype(jnp.bfloat16)
    return (attended, decode_pool)
```

```python
import itertools
import math

import jax
import jax.numpy as jnp
from jax import lax
from jax.sharding import PartitionSpec as P

MASKED = -1e30


def shortened(shard):
    return jax.tree.map(lambda a: a.astype(jnp.bfloat16) if a.dtype == jnp.float32 else a, shard)


def partner_2(value, axis, bit):
    mask = 2**bit
    pairs = [(source, source ^ mask) for source in range(lax.axis_size(axis))]
    return lax.ppermute(value, axis, pairs)


def page_partials(queries_at, key_rows, value_rows, token_mask):
    score_scale = 1.0 / math.sqrt(key_rows.shape[-1])
    scores = (
        jnp.einsum("nigex,ngpx->ngiep", queries_at, key_rows, preferred_element_type=jnp.float32)
        * score_scale
    )
    page_peak = jnp.max(jnp.where(token_mask, scores, MASKED), axis=-1)
    weights = jnp.where(token_mask, jnp.exp(scores - page_peak[..., None]), 0.0).astype(
        jnp.bfloat16
    )
    weight_sum = jnp.sum(weights.astype(jnp.float32), axis=-1)
    page_output = jnp.einsum(
        "ngiep,ngpx->ngiex", weights, value_rows, preferred_element_type=jnp.float32
    )
    return (page_peak, weight_sum, page_output)


def pick_where(take, partner, current):
    return tuple(
        (
            jnp.where(take.reshape((-1,) + (1,) * (own.ndim - 1)), other, own)
            for other, own in zip(partner, current)
        )
    )


def direct_routes(batch_count, positions):
    return math.comb(batch_count, positions) <= 128


def key_sets(batch_count, positions):
    chosen = list(itertools.combinations(range(batch_count), positions))
    return sorted(chosen, key=lambda keys: keys[::-1])


def set_index(route_keys, ranks, batch_count, positions):
    table = jnp.asarray(
        [[math.comb(key, rank + 1) for rank in range(positions)] for key in range(batch_count)],
        jnp.int32,
    )
    hits = (route_keys[:, None, None] == jnp.arange(batch_count)[None, :, None]) & (
        ranks[:, None, None] == jnp.arange(positions)[None, None, :]
    )
    return jnp.sum(jnp.where(hits, table[None], 0)).astype(jnp.int32)


def send_by(keys):
    def branch(pages):
        return tuple(
            page
            if key == 0
            else lax.ppermute(
                page, "batch", [(b, b ^ key) for b in range(lax.axis_size("batch"))]
            )
            for key, page in zip(keys, pages)
        )

    return branch


def choose(wanted, pages):
    picked = pages[0]
    for place in range(1, len(pages)):
        picked = jnp.where(wanted == place, pages[place], picked)
    return picked


def route_direct(send_pages, route_keys, batch_count, positions):
    ranks = jnp.sum((route_keys[None, :] < route_keys[:, None]).astype(jnp.int32), axis=1)
    slot_ids = jnp.arange(positions, dtype=jnp.int32)
    order = jnp.sum(
        jnp.where(ranks[None, :] == slot_ids[:, None], slot_ids[None, :], 0), axis=1
    )
    own = [send_pages[q] for q in range(positions)]
    ordered = tuple(choose(order[i], own) for i in range(positions))
    branches = [send_by(keys) for keys in key_sets(batch_count, positions)]
    arrived = lax.switch(
        set_index(route_keys, ranks, batch_count, positions), branches, ordered
    )
    return jnp.stack([choose(ranks[q], arrived) for q in range(positions)])


def on_device(prefill_cache, lengths, page_table, holder, queries, new_kv):
    batch_count, positions = holder.shape
    route_keys = holder[0]
    route_bits = lax.axis_size("batch").bit_length() - 1
    local_pages = lax.all_to_all(prefill_cache, "tensor", split_axis=3, concat_axis=1, tiled=True)[
        0
    ]
    kv_local, page_len, head_dim = (
        local_pages.shape[2],
        local_pages.shape[3],
        local_pages.shape[4],
    )
    owned_rows, layers, step_count = (queries.shape[0], queries.shape[1], queries.shape[2])
    group_size = queries.shape[3] // kv_local
    req_count, max_pages = page_table.shape
    layer_rows = lax.all_to_all(queries, "section", split_axis=1, concat_axis=0, tiled=True)
    local_queries = layer_rows[:, 0].reshape(req_count, step_count, kv_local, group_size, head_dim)
    slot_ids = jnp.arange(positions, dtype=jnp.int32)
    page_hits = (page_table[:, :, None] == slot_ids).astype(jnp.int32)
    in_use = jnp.sum(page_hits, axis=(0, 1)) > 0
    request_of = jnp.sum(
        page_hits * jnp.arange(req_count, dtype=jnp.int32)[:, None, None], axis=(0, 1)
    )
    page_of = jnp.sum(
        page_hits * jnp.arange(max_pages, dtype=jnp.int32)[None, :, None], axis=(0, 1)
    )
    length_of = jnp.sum(page_hits * lengths[:, None, None], axis=(0, 1))
    live_count = jnp.clip(length_of - page_of * page_len, 0, page_len)
    position_queries = jnp.take(local_queries, request_of, axis=0)
    send_pages = jnp.where(
        in_use[:, None, None, None, None], local_pages, jnp.zeros((), local_pages.dtype)
    )
    token_index = jnp.arange(page_len, dtype=jnp.int32)
    if direct_routes(batch_count, positions):
        decode_slots = route_direct(send_pages, route_keys, batch_count, positions)
    else:
        moving = (send_pages,)
        for bit in range(route_bits):
            take = route_keys // (1 << bit) % 2 == 1
            partner = jax.tree.map(
                lambda part, own: part.astype(own.dtype),
                partner_2(shortened(moving), "batch", bit),
                moving,
            )
            moving = pick_where(take, partner, moving)
        decode_slots = moving[0]
    token_mask = token_index[None, None, None, None, :] < live_count[:, None, None, None, None]
    page_peak, weight_sum, page_output = page_partials(
        position_queries, local_pages[:, 0], local_pages[:, 1], token_mask
    )
    mine = (request_of[None, :] == jnp.arange(req_count, dtype=jnp.int32)[:, None]) & in_use[
        None, :
    ]
    row_mask = mine[:, :, None, None, None]
    request_peak = jnp.max(jnp.where(row_mask, page_peak[None], MASKED), axis=1)
    factor = jnp.where(row_mask, jnp.exp(page_peak[None] - request_peak[:, None]), 0.0)
    numerator = jnp.einsum(
        "rqgie,qgiex->rgiex", factor, page_output, precision=lax.Precision.HIGHEST
    )
    denominator = jnp.sum(factor * weight_sum[None], axis=1)
    numerator, request_peak, denominator = (
        lax.all_to_all(numerator[:, None], "section", split_axis=0, concat_axis=1, tiled=True),
        lax.all_to_all(request_peak[:, None], "section", split_axis=0, concat_axis=1, tiled=True),
        lax.all_to_all(denominator[:, None], "section", split_axis=0, concat_axis=1, tiled=True),
    )
    flat_queries = queries.reshape(owned_rows * layers, step_count, kv_local, group_size, head_dim)
    new_keys = jnp.transpose(
        new_kv[:, :, :, 0].reshape(owned_rows * layers, step_count, kv_local, head_dim),
        (0, 2, 1, 3),
    )
    new_values = jnp.transpose(
        new_kv[:, :, :, 1].reshape(owned_rows * layers, step_count, kv_local, head_dim),
        (0, 2, 1, 3),
    )
    step_index = jnp.arange(step_count, dtype=jnp.int32)
    causal = step_index[None, :] <= step_index[:, None]
    new_peak, new_sum, new_output = page_partials(
        flat_queries, new_keys, new_values, causal[None, None, :, None, :]
    )
    new_peak = new_peak.reshape(request_peak.shape)
    new_sum = new_sum.reshape(denominator.shape)
    new_output = new_output.reshape(numerator.shape)
    joint_peak = jnp.maximum(request_peak, new_peak)
    old_scale = jnp.exp(request_peak - joint_peak)
    new_scale = jnp.exp(new_peak - joint_peak)
    result = (old_scale[..., None] * numerator + new_scale[..., None] * new_output) / (
        old_scale * denominator + new_scale * new_sum
    )[..., None]
    attended = (
        jnp.transpose(result, (0, 1, 3, 2, 4, 5))
        .reshape(owned_rows, layers, step_count, kv_local * group_size, head_dim)
        .astype(jnp.bfloat16)
    )
    return (attended, decode_slots.reshape((1,) + decode_slots.shape))


def solution(mesh):
    placed = (
        P("section", ("batch", "tensor"), None, None, None, None),
        P("batch"),
        P("batch", None),
        P(),
        P(("batch", "section"), None, None, "tensor", None),
        P(("batch", "section"), None, None, None, "tensor", None),
    )
    return jax.shard_map(
        on_device,
        mesh=mesh,
        in_specs=placed,
        out_specs=(
            P(("batch", "section"), None, None, "tensor", None),
            P("section", "batch", None, "tensor", None, None),
        ),
        check_vma=False,
    )
```

```python
import functools
import itertools
import math

import jax
import jax.numpy as jnp
from jax import lax
from jax.experimental import pallas as pl
from jax.experimental.pallas import tpu as pltpu
from jax.sharding import PartitionSpec as P

MASKED = -1e30


def shortened(shard):
    return jax.tree.map(lambda a: a.astype(jnp.bfloat16) if a.dtype == jnp.float32 else a, shard)


def partner_2(value, axis, bit):
    mask = 2**bit
    pairs = [(source, source ^ mask) for source in range(lax.axis_size(axis))]
    return lax.ppermute(value, axis, pairs)


def pick_where(take, partner, current):
    return tuple(
        (
            jnp.where(take.reshape((-1,) + (1,) * (own.ndim - 1)), other, own)
            for other, own in zip(partner, current)
        )
    )


def direct_routes(batch_count, positions):
    return math.comb(batch_count, positions) <= 128


def key_sets(batch_count, positions):
    chosen = list(itertools.combinations(range(batch_count), positions))
    return sorted(chosen, key=lambda keys: keys[::-1])


def set_index(route_keys, ranks, batch_count, positions):
    table = jnp.asarray(
        [[math.comb(key, rank + 1) for rank in range(positions)] for key in range(batch_count)],
        jnp.int32,
    )
    hits = (route_keys[:, None, None] == jnp.arange(batch_count)[None, :, None]) & (
        ranks[:, None, None] == jnp.arange(positions)[None, None, :]
    )
    return jnp.sum(jnp.where(hits, table[None], 0)).astype(jnp.int32)


def send_by(keys):
    def branch(pages):
        return tuple(
            page
            if key == 0
            else lax.ppermute(
                page, "batch", [(b, b ^ key) for b in range(lax.axis_size("batch"))]
            )
            for key, page in zip(keys, pages)
        )

    return branch


def choose(wanted, pages):
    picked = pages[0]
    for place in range(1, len(pages)):
        picked = jnp.where(wanted == place, pages[place], picked)
    return picked


def route_direct(ordered, route_keys, batch_count, positions):
    ranks = jnp.sum((route_keys[None, :] < route_keys[:, None]).astype(jnp.int32), axis=1)
    branches = [send_by(keys) for keys in key_sets(batch_count, positions)]
    arrived = lax.switch(
        set_index(route_keys, ranks, batch_count, positions), branches, tuple(ordered)
    )
    return jnp.stack([choose(ranks[q], arrived) for q in range(positions)])


MESH = pl.DeviceIdType.MESH


def rows_of(heads):
    wide = heads.astype(jnp.float32).reshape(-1, heads.shape[-1])
    return wide.astype(jnp.bfloat16)


def scores_of(query_rows, key_rows):
    product = lax.dot_general(
        query_rows, key_rows, (((1,), (1,)), ((), ())), preferred_element_type=jnp.float32
    )
    return product * (1.0 / math.sqrt(query_rows.shape[-1]))


def softmax_parts(scores, mask):
    peak = jnp.max(jnp.where(mask, scores, MASKED), axis=-1, keepdims=True)
    weights = jnp.where(mask, jnp.exp(scores - peak), 0.0).astype(jnp.bfloat16)
    total = jnp.sum(weights.astype(jnp.float32), axis=-1, keepdims=True)
    return peak, weights, total


def kernel(
    tensors, sections, batches, sort_pages,
    lengths, page_table, keys, cache, queries, new_rows,
    *rest,
):
    positions = keys.shape[1]
    ordered = rest[:positions]
    (attended, pages, layer_queries, page_out, page_peak, page_sum, new_out, new_peak, new_sum,
     outgoing, merged, load_sem, page_send, page_recv, query_sems, part_sems) = rest[positions:]
    tensor, section = lax.axis_index("tensor"), lax.axis_index("section")
    local_pages = cache.shape[1]
    kv_local = cache.shape[3] // tensors
    page_len, head = cache.shape[4], cache.shape[5]
    owned, layers, steps, heads = queries.shape[:4]
    requests = owned * sections
    group = heads // kv_local
    rows = steps * heads

    barrier = pltpu.get_barrier_semaphore()
    for ahead in range(1, tensors):
        other = lax.rem(tensor + ahead, tensors)
        pl.semaphore_signal(barrier, inc=1, device_id={"tensor": other}, device_id_type=MESH)
    for ahead in range(1, sections):
        other = lax.rem(section + ahead, sections)
        pl.semaphore_signal(barrier, inc=1, device_id={"section": other}, device_id_type=MESH)

    own_pages = pltpu.make_async_copy(
        cache.at[0, :, :, pl.ds(tensor * kv_local, kv_local)],
        pages.at[pl.ds(tensor * local_pages, local_pages)],
        load_sem.at[0],
    )
    own_pages.start()
    own_queries = pltpu.make_async_copy(
        queries.at[:, section], layer_queries.at[pl.ds(section * owned, owned)], load_sem.at[1]
    )
    own_queries.start()
    pl.semaphore_wait(barrier, tensors + sections - 2)

    query_copies = []
    for ahead in range(1, sections):
        other = lax.rem(section + ahead, sections)
        copy = pltpu.make_async_remote_copy(
            src_ref=queries.at[:, other],
            dst_ref=layer_queries.at[pl.ds(section * owned, owned)],
            send_sem=query_sems.at[0, ahead - 1],
            recv_sem=query_sems.at[1, ahead - 1],
            device_id={"section": other},
            device_id_type=MESH,
        )
        copy.start()
        query_copies.append(copy)
    page_copies = []
    for page in range(local_pages):
        for ahead in range(1, tensors):
            other = lax.rem(tensor + ahead, tensors)
            copy = pltpu.make_async_remote_copy(
                src_ref=cache.at[0, page, :, pl.ds(other * kv_local, kv_local)],
                dst_ref=pages.at[tensor * local_pages + page],
                send_sem=page_send.at[ahead - 1, page],
                recv_sem=page_recv.at[ahead - 1, page],
                device_id={"tensor": other},
                device_id_type=MESH,
            )
            copy.start()
            page_copies.append((page, ahead, copy))

    request_of, used, live = [], [], []
    for slot in range(positions):
        which, index, hits, length = 0, 0, 0, 0
        for row in range(requests):
            for column in range(page_table.shape[1]):
                hit = (page_table[row, column] == slot).astype(jnp.int32)
                hits += hit
                which += hit * row
                index += hit * column
                length += hit * lengths[row]
        request_of.append(jnp.minimum(which, requests - 1))
        used.append(hits)
        live.append(jnp.clip(length - index * page_len, 0, page_len) * (hits > 0).astype(jnp.int32))

    def at_slot(values, slot):
        picked = values[0]
        for place in range(1, positions):
            picked = jnp.where(slot == place, values[place], picked)
        return picked

    row_ids = lax.broadcasted_iota(jnp.int32, (rows, 1), 0)
    row_head = lax.rem(row_ids, heads) // group
    row_step = row_ids // heads

    columns = new_rows.shape[2]
    column_ids = lax.broadcasted_iota(jnp.int32, (1, columns), 1)
    new_mask = (
        (lax.rem(column_ids, 2 * kv_local) == row_head)
        & (column_ids // (2 * kv_local) <= row_step)
    )
    for mine in range(owned):
        for layer in range(layers):
            new = new_rows[mine, layer]
            scores = scores_of(rows_of(queries[mine, layer]), new)
            peak, weights, total = softmax_parts(scores, new_mask)
            wide = new.astype(jnp.float32)
            values = jnp.concatenate([wide[kv_local:], wide[:kv_local]], axis=0)
            new_out[mine, layer] = jnp.dot(
                weights, values.astype(jnp.bfloat16), preferred_element_type=jnp.float32
            )
            new_peak[mine, layer] = jnp.broadcast_to(peak, (rows, head))
            new_sum[mine, layer] = jnp.broadcast_to(total, (rows, head))

    own_queries.wait()
    for copy in query_copies:
        copy.wait()
    own_pages.wait()

    token_ids = lax.broadcasted_iota(jnp.int32, (1, page_len), 1)

    def attend(slot):
        query_rows = rows_of(layer_queries[at_slot(request_of, slot)])
        scores = scores_of(query_rows, pages[slot, 0, 0])
        for place in range(1, kv_local):
            scores = jnp.where(
                row_head == place, scores_of(query_rows, pages[slot, 0, place]), scores
            )
        peak, weights, total = softmax_parts(scores, token_ids < at_slot(live, slot))
        out = jnp.dot(weights, pages[slot, 1, 0], preferred_element_type=jnp.float32)
        for place in range(1, kv_local):
            out = jnp.where(
                row_head == place,
                jnp.dot(weights, pages[slot, 1, place], preferred_element_type=jnp.float32),
                out,
            )
        page_out[slot] = out
        page_peak[slot] = jnp.broadcast_to(peak, (rows, head))
        page_sum[slot] = jnp.broadcast_to(total, (rows, head))

    for page in range(local_pages):
        attend(tensor * local_pages + page)
    for page, ahead, copy in page_copies:
        copy.wait_recv()
        attend(lax.rem(tensor + tensors - ahead, tensors) * local_pages + page)

    lane = lax.broadcasted_iota(jnp.int32, (rows, head), 1)

    def merge(request):
        takes = [
            (request_of[slot] == request) & (used[slot] > 0) for slot in range(positions)
        ]
        top = jnp.full((rows, head), MASKED, jnp.float32)
        for slot in range(positions):
            top = jnp.maximum(top, jnp.where(takes[slot], page_peak[slot], MASKED))
        numerator = jnp.zeros((rows, head), jnp.float32)
        denominator = jnp.zeros((rows, head), jnp.float32)
        for slot in range(positions):
            factor = jnp.where(takes[slot], jnp.exp(page_peak[slot] - top), 0.0)
            numerator += factor * page_out[slot]
            denominator += factor * page_sum[slot]
        return numerator, jnp.where(lane < head // 2, top, denominator)

    part_copies = []
    for ahead in range(1, sections):
        other = lax.rem(section + ahead, sections)
        for mine in range(owned):
            numerator, stats = merge(other * owned + mine)
            outgoing[ahead - 1, mine, 0] = numerator
            outgoing[ahead - 1, mine, 1] = stats
        copy = pltpu.make_async_remote_copy(
            src_ref=outgoing.at[ahead - 1],
            dst_ref=merged.at[section],
            send_sem=part_sems.at[0, ahead - 1],
            recv_sem=part_sems.at[1, ahead - 1],
            device_id={"section": other},
            device_id_type=MESH,
        )
        copy.start()
        part_copies.append(copy)
    for mine in range(owned):
        numerator, stats = merge(section * owned + mine)
        merged[section, mine, 0] = numerator
        merged[section, mine, 1] = stats

    ranks = []
    for slot in range(positions):
        below = 0
        for other in range(positions):
            below += (keys[0, other] < keys[0, slot]).astype(jnp.int32)
        ranks.append(below if sort_pages else slot)
    for place in range(positions):
        slot, keep = 0, 0
        for q in range(positions):
            if sort_pages:
                hit = (ranks[q] == place).astype(jnp.int32)
                slot += hit * q
                keep += hit * used[q]
            elif q == place:
                slot, keep = q, used[q]
        slot = jnp.minimum(slot, positions - 1)
        for entry in range(2):
            for place_head in range(kv_local):
                page = pages[slot, entry, place_head]
                ordered[place][entry, place_head] = lax.select(
                    keep > 0, page, jnp.zeros_like(page)
                )

    for copy in part_copies:
        copy.wait()
    for mine in range(owned):
        for layer in range(layers):
            numerator, stats = merged[layer, mine, 0], merged[layer, mine, 1]
            top, denominator = stats[:, :1], stats[:, head // 2 : head // 2 + 1]
            latest = new_peak[mine, layer]
            joint = jnp.maximum(top, latest)
            old_scale, new_scale = jnp.exp(top - joint), jnp.exp(latest - joint)
            result = (old_scale * numerator + new_scale * new_out[mine, layer]) / (
                old_scale * denominator + new_scale * new_sum[mine, layer]
            )
            attended[mine, layer] = result.reshape(steps, heads, head).astype(jnp.bfloat16)
    for _, _, copy in page_copies:
        copy.wait_send()


def attend_and_order(prefill_cache, lengths, page_table, holder, queries, new_kv, sort_pages):
    tensors, sections = lax.axis_size("tensor"), lax.axis_size("section")
    batches, positions = holder.shape
    local_pages, cache_heads, page_len, head = (
        prefill_cache.shape[1],
        prefill_cache.shape[3],
        prefill_cache.shape[4],
        prefill_cache.shape[5],
    )
    kv_local = cache_heads // tensors
    owned, layers, steps, heads = queries.shape[:4]
    rows = steps * heads
    new_rows = new_kv.reshape(owned, layers, steps * 2 * kv_local, head)
    page = jax.ShapeDtypeStruct((2, kv_local, page_len, head), jnp.bfloat16)
    smem = pl.BlockSpec(memory_space=pltpu.SMEM)
    vmem = pl.BlockSpec(memory_space=pltpu.VMEM)

    def wide(*lead):
        return pltpu.VMEM(lead + (rows, head), jnp.float32)

    result = pl.pallas_call(
        functools.partial(kernel, tensors, sections, batches, sort_pages),
        out_shape=[page] * positions + [jax.ShapeDtypeStruct(queries.shape, jnp.bfloat16)],
        in_specs=[smem, smem, smem, pl.BlockSpec(memory_space=pl.ANY), vmem, vmem],
        out_specs=[vmem] * (positions + 1),
        scratch_shapes=[
            pltpu.VMEM((positions, 2, kv_local, page_len, head), jnp.bfloat16),
            pltpu.VMEM((owned * sections, steps, heads, head), jnp.bfloat16),
            wide(positions), wide(positions), wide(positions),
            wide(owned, layers), wide(owned, layers), wide(owned, layers),
            wide(max(sections - 1, 1), owned, 2),
            wide(sections, owned, 2),
            pltpu.SemaphoreType.DMA((2,)),
            pltpu.SemaphoreType.DMA((max(tensors - 1, 1), local_pages)),
            pltpu.SemaphoreType.DMA((max(tensors - 1, 1), local_pages)),
            pltpu.SemaphoreType.DMA((2, max(sections - 1, 1))),
            pltpu.SemaphoreType.DMA((2, max(sections - 1, 1))),
        ],
        compiler_params=pltpu.CompilerParams(collective_id=0, has_side_effects=True),
        name="attend_and_order",
    )(lengths, page_table, holder, prefill_cache, queries, new_rows)
    return result[:positions], result[positions]


def on_device(prefill_cache, lengths, page_table, holder, queries, new_kv):
    batch_count, positions = holder.shape
    route_keys = holder[0]
    direct = direct_routes(batch_count, positions)
    pages, attended = attend_and_order(
        prefill_cache, lengths, page_table, holder, queries, new_kv, direct
    )
    if direct:
        decode_slots = route_direct(pages, route_keys, batch_count, positions)
    else:
        moving = (jnp.stack(pages),)
        for bit in range(lax.axis_size("batch").bit_length() - 1):
            take = route_keys // (1 << bit) % 2 == 1
            partner = jax.tree.map(
                lambda part, own: part.astype(own.dtype),
                partner_2(shortened(moving), "batch", bit),
                moving,
            )
            moving = pick_where(take, partner, moving)
        decode_slots = moving[0]
    return (attended, decode_slots.reshape((1,) + decode_slots.shape))


def solution(mesh):
    placed = (
        P("section", ("batch", "tensor"), None, None, None, None),
        P("batch"),
        P("batch", None),
        P(),
        P(("batch", "section"), None, None, "tensor", None),
        P(("batch", "section"), None, None, None, "tensor", None),
    )
    return jax.shard_map(
        on_device,
        mesh=mesh,
        in_specs=placed,
        out_specs=(
            P(("batch", "section"), None, None, "tensor", None),
            P("section", "batch", None, "tensor", None, None),
        ),
        check_vma=False,
    )
```

```python
import functools
import math

import jax
import jax.numpy as jnp
from jax import lax
from jax.experimental import pallas as pl
from jax.experimental.pallas import tpu as pltpu
from jax.sharding import PartitionSpec as P

MASKED = -1e30


def shortened(shard):
    return jax.tree.map(lambda a: a.astype(jnp.bfloat16) if a.dtype == jnp.float32 else a, shard)


def partner_2(value, axis, bit):
    mask = 2**bit
    pairs = [(source, source ^ mask) for source in range(lax.axis_size(axis))]
    return lax.ppermute(value, axis, pairs)


def pick_where(take, partner, current):
    return tuple(
        (
            jnp.where(take.reshape((-1,) + (1,) * (own.ndim - 1)), other, own)
            for other, own in zip(partner, current)
        )
    )


def sends_by_key(batch_count, positions):
    return batch_count % 4 == 0 and batch_count <= 2 * positions


def exclusive_or(value, mask, count):
    total = 0
    bit = 1
    while bit < count:
        total = total + lax.rem(value // bit + mask // bit % 2, 2) * bit
        bit *= 2
    return total


MESH = pl.DeviceIdType.MESH


def rows_of(heads):
    wide = heads.astype(jnp.float32).reshape(-1, heads.shape[-1])
    return wide.astype(jnp.bfloat16)


def scores_of(query_rows, key_rows):
    product = lax.dot_general(
        query_rows, key_rows, (((1,), (1,)), ((), ())), preferred_element_type=jnp.float32
    )
    return product * (1.0 / math.sqrt(query_rows.shape[-1]))


def softmax_parts(scores, mask):
    peak = jnp.max(jnp.where(mask, scores, MASKED), axis=-1, keepdims=True)
    weights = jnp.where(mask, jnp.exp(scores - peak), 0.0).astype(jnp.bfloat16)
    total = jnp.sum(weights.astype(jnp.float32), axis=-1, keepdims=True)
    return peak, weights, total


def kernel(
    tensors, sections, batches, by_key,
    lengths, page_table, keys, cache, queries, new_rows,
    *rest,
):
    positions = keys.shape[0]
    outs = 1 if by_key else positions
    slots_out = rest[:outs]
    attended, rest = rest[outs], rest[outs + 1 :]
    kv_local = cache.shape[3] // tensors
    chunks = [(entry, place) for entry in range(2) for place in range(kv_local)]
    pages, rest = rest[: len(chunks)], rest[len(chunks) :]
    (layer_queries, page_out, page_peak, page_sum, new_out, new_peak, new_sum,
     outgoing, merged, load_sem, page_send, page_recv, query_sems, part_sems) = rest[:14]
    if by_key:
        leaving, passing, key_send, key_recv, pass_send, pass_recv, on_send = rest[14:21]
        landing = rest[21:]
    tensor, section = lax.axis_index("tensor"), lax.axis_index("section")
    batch = lax.axis_index("batch")
    local_pages = cache.shape[1]
    page_len, head = cache.shape[4], cache.shape[5]
    owned, layers, steps, heads = queries.shape[:4]
    requests = owned * sections
    columns_of = page_table.shape[0] // requests
    group = heads // kv_local
    rows = steps * heads

    quarter = max(batches // 4, 1)
    stretch, offset = batch // quarter, lax.rem(batch, quarter)
    up = lax.rem(stretch + 1, 4) * quarter + offset
    down = lax.rem(stretch + 3, 4) * quarter + offset

    barrier = pltpu.get_barrier_semaphore()
    greeted = 0
    for ahead in range(1, tensors):
        other = lax.rem(tensor + ahead, tensors)
        pl.semaphore_signal(barrier, inc=1, device_id={"tensor": other}, device_id_type=MESH)
        greeted += 1
    for ahead in range(1, sections):
        other = lax.rem(section + ahead, sections)
        pl.semaphore_signal(barrier, inc=1, device_id={"section": other}, device_id_type=MESH)
        greeted += 1
    if by_key:
        for key in range(1, batches):
            other = exclusive_or(batch, key, batches)
            pl.semaphore_signal(barrier, inc=1, device_id={"batch": other}, device_id_type=MESH)
            greeted += 1

    own_pages = []
    for chunk, (entry, place) in enumerate(chunks):
        copy = pltpu.make_async_copy(
            cache.at[0, :, entry, tensor * kv_local + place],
            pages[chunk].at[pl.ds(tensor * local_pages, local_pages)],
            load_sem.at[1 + chunk],
        )
        copy.start()
        own_pages.append(copy)
    own_queries = pltpu.make_async_copy(
        queries.at[:, section], layer_queries.at[pl.ds(section * owned, owned)], load_sem.at[0]
    )
    own_queries.start()
    pl.semaphore_wait(barrier, greeted)

    page_copies = []
    for chunk, (entry, place) in enumerate(chunks):
        copies = []
        for page in range(local_pages):
            for ahead in range(1, tensors):
                other = lax.rem(tensor + ahead, tensors)
                copy = pltpu.make_async_remote_copy(
                    src_ref=cache.at[0, page, entry, other * kv_local + place],
                    dst_ref=pages[chunk].at[tensor * local_pages + page],
                    send_sem=page_send.at[ahead - 1, page, chunk],
                    recv_sem=page_recv.at[ahead - 1, page, chunk],
                    device_id={"tensor": other},
                    device_id_type=MESH,
                )
                copy.start()
                copies.append(copy)
        page_copies.append(copies)
    query_copies = []
    for ahead in range(1, sections):
        other = lax.rem(section + ahead, sections)
        copy = pltpu.make_async_remote_copy(
            src_ref=queries.at[:, other],
            dst_ref=layer_queries.at[pl.ds(section * owned, owned)],
            send_sem=query_sems.at[0, ahead - 1],
            recv_sem=query_sems.at[1, ahead - 1],
            device_id={"section": other},
            device_id_type=MESH,
        )
        copy.start()
        query_copies.append(copy)

    request_of, used, live = [], [], []
    for slot in range(positions):
        which, index, hits, length = 0, 0, 0, 0
        for row in range(requests):
            for column in range(columns_of):
                hit = (page_table[row * columns_of + column] == slot).astype(jnp.int32)
                hits += hit
                which += hit * row
                index += hit * column
                length += hit * lengths[row]
        request_of.append(jnp.minimum(which, requests - 1))
        used.append(hits)
        live.append(jnp.clip(length - index * page_len, 0, page_len) * (hits > 0).astype(jnp.int32))

    def at_slot(values, slot):
        picked = values[0]
        for place in range(1, positions):
            picked = jnp.where(slot == place, values[place], picked)
        return picked

    row_ids = lax.broadcasted_iota(jnp.int32, (rows, 1), 0)
    row_head = lax.rem(row_ids, heads) // group
    row_step = row_ids // heads

    columns = new_rows.shape[2]
    column_ids = lax.broadcasted_iota(jnp.int32, (1, columns), 1)
    new_mask = (
        (lax.rem(column_ids, 2 * kv_local) == row_head)
        & (column_ids // (2 * kv_local) <= row_step)
    )
    for mine in range(owned):
        for layer in range(layers):
            new = new_rows[mine, layer]
            scores = scores_of(rows_of(queries[mine, layer]), new)
            peak, weights, total = softmax_parts(scores, new_mask)
            wide = new.astype(jnp.float32)
            values = jnp.concatenate([wide[kv_local:], wide[:kv_local]], axis=0)
            new_out[mine, layer] = jnp.dot(
                weights, values.astype(jnp.bfloat16), preferred_element_type=jnp.float32
            )
            new_peak[mine, layer] = jnp.broadcast_to(peak, (rows, head))
            new_sum[mine, layer] = jnp.broadcast_to(total, (rows, head))

    own_queries.wait()
    for copy in query_copies:
        copy.wait()
    for copy in own_pages:
        copy.wait()

    token_ids = lax.broadcasted_iota(jnp.int32, (1, page_len), 1)

    def attend(slot):
        query_rows = rows_of(layer_queries[at_slot(request_of, slot)])
        scores = scores_of(query_rows, pages[0][slot])
        for place in range(1, kv_local):
            scores = jnp.where(
                row_head == place, scores_of(query_rows, pages[place][slot]), scores
            )
        peak, weights, total = softmax_parts(scores, token_ids < at_slot(live, slot))
        out = jnp.dot(weights, pages[kv_local][slot], preferred_element_type=jnp.float32)
        for place in range(1, kv_local):
            out = jnp.where(
                row_head == place,
                jnp.dot(weights, pages[kv_local + place][slot], preferred_element_type=jnp.float32),
                out,
            )
        page_out[slot] = out
        page_peak[slot] = jnp.broadcast_to(peak, (rows, head))
        page_sum[slot] = jnp.broadcast_to(total, (rows, head))

    def page_for(key):
        slot, keep = 0, 0
        for q in range(positions):
            hit = (keys[q] == key).astype(jnp.int32)
            slot += hit * q
            keep += hit * used[q]
        return jnp.minimum(slot, positions - 1), keep

    halves = batches // 2
    passed = [key for key in range(halves, halves + quarter)] if by_key else []
    straight = [key for key in range(1, batches) if key not in passed] if by_key else []
    sources = [page_for(key) for key in range(batches)] if by_key else []
    straight_copies = [[] for _ in chunks]
    first_copies = [[] for _ in chunks]
    second_copies = [[] for _ in chunks]

    def send(chunk, entry, place):
        for key in passed + straight + [0]:
            slot, keep = sources[key]
            page = pages[chunk][slot]
            page = lax.select(keep > 0, page, jnp.zeros_like(page))
            if key == 0:
                landing[chunk][0] = page
                continue
            leaving[key, chunk] = page
            if key in passed:
                turn = key - halves
                copy = pltpu.make_async_remote_copy(
                    src_ref=leaving.at[key, chunk],
                    dst_ref=passing.at[turn, chunk],
                    send_sem=pass_send.at[turn, chunk],
                    recv_sem=pass_recv.at[turn, chunk],
                    device_id={"batch": down if turn % 2 else up},
                    device_id_type=MESH,
                )
                first_copies[chunk].append(copy)
            else:
                copy = pltpu.make_async_remote_copy(
                    src_ref=leaving.at[key, chunk],
                    dst_ref=landing[chunk].at[key],
                    send_sem=key_send.at[key, chunk],
                    recv_sem=key_recv.at[key, chunk],
                    device_id={"batch": exclusive_or(batch, key, batches)},
                    device_id_type=MESH,
                )
                straight_copies[chunk].append(copy)
            copy.start()

    def pass_on(chunk):
        for turn, first in enumerate(first_copies[chunk]):
            first.wait_recv()
            onward = exclusive_or(down if turn % 2 else up, turn, batches)
            copy = pltpu.make_async_remote_copy(
                src_ref=passing.at[turn, chunk],
                dst_ref=landing[chunk].at[halves + turn],
                send_sem=on_send.at[turn, chunk],
                recv_sem=key_recv.at[halves + turn, chunk],
                device_id={"batch": onward},
                device_id_type=MESH,
            )
            copy.start()
            second_copies[chunk].append(copy)

    for chunk, (entry, place) in enumerate(chunks):
        for copy in page_copies[chunk]:
            copy.wait_recv()
        if by_key:
            send(chunk, entry, place)
        if chunk < local_pages:
            attend(tensor * local_pages + chunk)
        if by_key and chunk > 0:
            pass_on(chunk - 1)
    for page in range(len(chunks), local_pages):
        attend(tensor * local_pages + page)
    for page in range(local_pages):
        for ahead in range(1, tensors):
            attend(lax.rem(tensor + tensors - ahead, tensors) * local_pages + page)

    lane = lax.broadcasted_iota(jnp.int32, (rows, head), 1)

    def merge(request):
        takes = [
            (request_of[slot] == request) & (used[slot] > 0) for slot in range(positions)
        ]
        top = jnp.full((rows, head), MASKED, jnp.float32)
        for slot in range(positions):
            top = jnp.maximum(top, jnp.where(takes[slot], page_peak[slot], MASKED))
        numerator = jnp.zeros((rows, head), jnp.float32)
        denominator = jnp.zeros((rows, head), jnp.float32)
        for slot in range(positions):
            factor = jnp.where(takes[slot], jnp.exp(page_peak[slot] - top), 0.0)
            numerator += factor * page_out[slot]
            denominator += factor * page_sum[slot]
        return numerator, jnp.where(lane < head // 2, top, denominator)

    part_copies = []
    for ahead in range(1, sections):
        other = lax.rem(section + ahead, sections)
        for mine in range(owned):
            numerator, stats = merge(other * owned + mine)
            outgoing[ahead - 1, mine, 0] = numerator
            outgoing[ahead - 1, mine, 1] = stats
        copy = pltpu.make_async_remote_copy(
            src_ref=outgoing.at[ahead - 1],
            dst_ref=merged.at[section],
            send_sem=part_sems.at[0, ahead - 1],
            recv_sem=part_sems.at[1, ahead - 1],
            device_id={"section": other},
            device_id_type=MESH,
        )
        copy.start()
        part_copies.append(copy)
    for mine in range(owned):
        numerator, stats = merge(section * owned + mine)
        merged[section, mine, 0] = numerator
        merged[section, mine, 1] = stats

    if by_key:
        pass_on(len(chunks) - 1)
    else:
        for slot in range(positions):
            for chunk, (entry, place) in enumerate(chunks):
                page = pages[chunk][slot]
                slots_out[slot][entry, place] = lax.select(
                    used[slot] > 0, page, jnp.zeros_like(page)
                )

    for copy in part_copies:
        copy.wait()
    for mine in range(owned):
        for layer in range(layers):
            numerator, stats = merged[layer, mine, 0], merged[layer, mine, 1]
            top, denominator = stats[:, :1], stats[:, head // 2 : head // 2 + 1]
            latest = new_peak[mine, layer]
            joint = jnp.maximum(top, latest)
            old_scale, new_scale = jnp.exp(top - joint), jnp.exp(latest - joint)
            result = (old_scale * numerator + new_scale * new_out[mine, layer]) / (
                old_scale * denominator + new_scale * new_sum[mine, layer]
            )
            attended[mine, layer] = result.reshape(steps, heads, head).astype(jnp.bfloat16)
    for chunk, (entry, place) in enumerate(chunks):
        if by_key:
            for copy in straight_copies[chunk] + second_copies[chunk]:
                copy.wait_recv()
            for slot in range(positions):
                slots_out[0][slot, entry, place] = landing[chunk][
                    jnp.minimum(keys[slot], batches - 1)
                ]
    for chunk in range(len(chunks)):
        for copy in (
            page_copies[chunk] + straight_copies[chunk] + first_copies[chunk]
            + second_copies[chunk]
        ):
            copy.wait_send()


def attend_and_order(prefill_cache, lengths, page_table, holder, queries, new_kv, by_key):
    tensors, sections = lax.axis_size("tensor"), lax.axis_size("section")
    batches, positions = holder.shape
    local_pages, cache_heads, page_len, head = (
        prefill_cache.shape[1],
        prefill_cache.shape[3],
        prefill_cache.shape[4],
        prefill_cache.shape[5],
    )
    kv_local = cache_heads // tensors
    owned, layers, steps, heads = queries.shape[:4]
    rows = steps * heads
    new_rows = new_kv.reshape(owned, layers, steps * 2 * kv_local, head)
    page = jax.ShapeDtypeStruct((2, kv_local, page_len, head), jnp.bfloat16)
    smem = pl.BlockSpec(memory_space=pltpu.SMEM)
    vmem = pl.BlockSpec(memory_space=pltpu.VMEM)

    def wide(*lead):
        return pltpu.VMEM(lead + (rows, head), jnp.float32)

    if by_key:
        outs = [jax.ShapeDtypeStruct((positions,) + page.shape, page.dtype)]
        turns = batches // 4
        key_scratch = [
            pltpu.VMEM((batches, 2 * kv_local, page_len, head), jnp.bfloat16),
            pltpu.VMEM((turns, 2 * kv_local, page_len, head), jnp.bfloat16),
            pltpu.SemaphoreType.DMA((batches, 2 * kv_local)),
            pltpu.SemaphoreType.DMA((batches, 2 * kv_local)),
            pltpu.SemaphoreType.DMA((turns, 2 * kv_local)),
            pltpu.SemaphoreType.DMA((turns, 2 * kv_local)),
            pltpu.SemaphoreType.DMA((turns, 2 * kv_local)),
            *[pltpu.VMEM((batches, page_len, head), jnp.bfloat16)] * (2 * kv_local),
        ]
    else:
        outs, key_scratch = [page] * positions, []
    result = pl.pallas_call(
        functools.partial(kernel, tensors, sections, batches, by_key),
        out_shape=outs + [jax.ShapeDtypeStruct(queries.shape, jnp.bfloat16)],
        in_specs=[smem, smem, smem, pl.BlockSpec(memory_space=pl.ANY), vmem, vmem],
        out_specs=[vmem] * (len(outs) + 1),
        scratch_shapes=[
            *[pltpu.VMEM((positions, page_len, head), jnp.bfloat16)] * (2 * kv_local),
            pltpu.VMEM((owned * sections, steps, heads, head), jnp.bfloat16),
            wide(positions), wide(positions), wide(positions),
            wide(owned, layers), wide(owned, layers), wide(owned, layers),
            wide(max(sections - 1, 1), owned, 2),
            wide(sections, owned, 2),
            pltpu.SemaphoreType.DMA((1 + 2 * kv_local,)),
            pltpu.SemaphoreType.DMA((max(tensors - 1, 1), local_pages, 2 * kv_local)),
            pltpu.SemaphoreType.DMA((max(tensors - 1, 1), local_pages, 2 * kv_local)),
            pltpu.SemaphoreType.DMA((2, max(sections - 1, 1))),
            pltpu.SemaphoreType.DMA((2, max(sections - 1, 1))),
        ] + key_scratch,
        compiler_params=pltpu.CompilerParams(collective_id=0, has_side_effects=True),
        name="attend_and_order",
    )(lengths, page_table.reshape(-1), holder[0], prefill_cache, queries, new_rows)
    return result[:-1], result[-1]


def on_device(prefill_cache, lengths, page_table, holder, queries, new_kv):
    batch_count, positions = holder.shape
    route_keys = holder[0]
    by_key = sends_by_key(batch_count, positions)
    pages, attended = attend_and_order(
        prefill_cache, lengths, page_table, holder, queries, new_kv, by_key
    )
    if by_key:
        decode_slots = pages[0]
    else:
        moving = (jnp.stack(pages),)
        for bit in range(lax.axis_size("batch").bit_length() - 1):
            take = route_keys // (1 << bit) % 2 == 1
            partner = jax.tree.map(
                lambda part, own: part.astype(own.dtype),
                partner_2(shortened(moving), "batch", bit),
                moving,
            )
            moving = pick_where(take, partner, moving)
        decode_slots = moving[0]
    return (attended, decode_slots.reshape((1,) + decode_slots.shape))


def solution(mesh):
    placed = (
        P("section", ("batch", "tensor"), None, None, None, None),
        P("batch"),
        P("batch", None),
        P(),
        P(("batch", "section"), None, None, "tensor", None),
        P(("batch", "section"), None, None, None, "tensor", None),
    )
    return jax.shard_map(
        on_device,
        mesh=mesh,
        in_specs=placed,
        out_specs=(
            P(("batch", "section"), None, None, "tensor", None),
            P("section", "batch", None, "tensor", None, None),
        ),
        check_vma=False,
    )
```

```python
import functools
import math

import jax
import jax.numpy as jnp
from jax import lax
from jax.experimental import pallas as pl
from jax.experimental.pallas import tpu as pltpu
from jax.sharding import PartitionSpec as P

MASKED = -1e30


def shortened(shard):
    return jax.tree.map(lambda a: a.astype(jnp.bfloat16) if a.dtype == jnp.float32 else a, shard)


def partner_2(value, axis, bit):
    mask = 2**bit
    pairs = [(source, source ^ mask) for source in range(lax.axis_size(axis))]
    return lax.ppermute(value, axis, pairs)


def pick_where(take, partner, current):
    return tuple(
        (
            jnp.where(take.reshape((-1,) + (1,) * (own.ndim - 1)), other, own)
            for other, own in zip(partner, current)
        )
    )


def sends_by_key(batch_count, positions):
    return batch_count % 4 == 0 and batch_count <= 2 * positions


def exclusive_or(value, mask, count):
    total = 0
    bit = 1
    while bit < count:
        total = total + lax.rem(value // bit + mask // bit % 2, 2) * bit
        bit *= 2
    return total


MESH = pl.DeviceIdType.MESH


def rows_of(heads):
    wide = heads.astype(jnp.float32).reshape(-1, heads.shape[-1])
    return wide.astype(jnp.bfloat16)


def scores_of(query_rows, key_rows):
    product = lax.dot_general(
        query_rows, key_rows, (((1,), (1,)), ((), ())), preferred_element_type=jnp.float32
    )
    return product * (1.0 / math.sqrt(query_rows.shape[-1]))


def softmax_parts(scores, mask):
    peak = jnp.max(jnp.where(mask, scores, MASKED), axis=-1, keepdims=True)
    weights = jnp.where(mask, jnp.exp(scores - peak), 0.0).astype(jnp.bfloat16)
    total = jnp.sum(weights.astype(jnp.float32), axis=-1, keepdims=True)
    return peak, weights, total


def kernel(
    tensors, sections, batches, sent_keys,
    lengths, page_table, keys, cache, queries, new_rows,
    *rest,
):
    positions = keys.shape[0]
    by_key = sent_keys is not None
    outs = 1 if by_key else positions
    slots_out = rest[:outs]
    attended, rest = rest[outs], rest[outs + 1 :]
    kv_local = cache.shape[3] // tensors
    chunks = [(entry, place) for entry in range(2) for place in range(kv_local)]
    pages, rest = rest[: len(chunks)], rest[len(chunks) :]
    (layer_queries, page_out, page_peak, page_sum, new_out, new_peak, new_sum,
     outgoing, merged, load_sem, page_send, page_recv, query_sems, part_sems) = rest[:14]
    if by_key:
        leaving, key_send, key_recv = rest[14:17]
        landing = rest[17:]
    tensor, section = lax.axis_index("tensor"), lax.axis_index("section")
    batch = lax.axis_index("batch")
    local_pages = cache.shape[1]
    page_len, head = cache.shape[4], cache.shape[5]
    owned, layers, steps, heads = queries.shape[:4]
    requests = owned * sections
    columns_of = page_table.shape[0] // requests
    group = heads // kv_local
    rows = steps * heads

    barrier = pltpu.get_barrier_semaphore()
    greeted = 0
    for ahead in range(1, tensors):
        other = lax.rem(tensor + ahead, tensors)
        pl.semaphore_signal(barrier, inc=1, device_id={"tensor": other}, device_id_type=MESH)
        greeted += 1
    for ahead in range(1, sections):
        other = lax.rem(section + ahead, sections)
        pl.semaphore_signal(barrier, inc=1, device_id={"section": other}, device_id_type=MESH)
        greeted += 1
    if by_key:
        for key in sent_keys:
            other = exclusive_or(batch, key, batches)
            pl.semaphore_signal(barrier, inc=1, device_id={"batch": other}, device_id_type=MESH)
            greeted += 1

    own_pages = []
    for chunk, (entry, place) in enumerate(chunks):
        copy = pltpu.make_async_copy(
            cache.at[0, :, entry, tensor * kv_local + place],
            pages[chunk].at[pl.ds(tensor * local_pages, local_pages)],
            load_sem.at[1 + chunk],
        )
        copy.start()
        own_pages.append(copy)
    own_queries = pltpu.make_async_copy(
        queries.at[:, section], layer_queries.at[pl.ds(section * owned, owned)], load_sem.at[0]
    )
    own_queries.start()
    pl.semaphore_wait(barrier, greeted)

    page_copies = []
    for chunk, (entry, place) in enumerate(chunks):
        copies = []
        for page in range(local_pages):
            for ahead in range(1, tensors):
                other = lax.rem(tensor + ahead, tensors)
                copy = pltpu.make_async_remote_copy(
                    src_ref=cache.at[0, page, entry, other * kv_local + place],
                    dst_ref=pages[chunk].at[tensor * local_pages + page],
                    send_sem=page_send.at[ahead - 1, page, chunk],
                    recv_sem=page_recv.at[ahead - 1, page, chunk],
                    device_id={"tensor": other},
                    device_id_type=MESH,
                )
                copy.start()
                copies.append(copy)
        page_copies.append(copies)
    query_copies = []
    for ahead in range(1, sections):
        other = lax.rem(section + ahead, sections)
        copy = pltpu.make_async_remote_copy(
            src_ref=queries.at[:, other],
            dst_ref=layer_queries.at[pl.ds(section * owned, owned)],
            send_sem=query_sems.at[0, ahead - 1],
            recv_sem=query_sems.at[1, ahead - 1],
            device_id={"section": other},
            device_id_type=MESH,
        )
        copy.start()
        query_copies.append(copy)

    request_of, used, live = [], [], []
    for slot in range(positions):
        which, index, hits, length = 0, 0, 0, 0
        for row in range(requests):
            for column in range(columns_of):
                hit = (page_table[row * columns_of + column] == slot).astype(jnp.int32)
                hits += hit
                which += hit * row
                index += hit * column
                length += hit * lengths[row]
        request_of.append(jnp.minimum(which, requests - 1))
        used.append(hits)
        live.append(jnp.clip(length - index * page_len, 0, page_len) * (hits > 0).astype(jnp.int32))

    def at_slot(values, slot):
        picked = values[0]
        for place in range(1, positions):
            picked = jnp.where(slot == place, values[place], picked)
        return picked

    row_ids = lax.broadcasted_iota(jnp.int32, (rows, 1), 0)
    row_head = lax.rem(row_ids, heads) // group
    row_step = row_ids // heads

    columns = new_rows.shape[2]
    column_ids = lax.broadcasted_iota(jnp.int32, (1, columns), 1)
    new_mask = (
        (lax.rem(column_ids, 2 * kv_local) == row_head)
        & (column_ids // (2 * kv_local) <= row_step)
    )
    for mine in range(owned):
        for layer in range(layers):
            new = new_rows[mine, layer]
            scores = scores_of(rows_of(queries[mine, layer]), new)
            peak, weights, total = softmax_parts(scores, new_mask)
            wide = new.astype(jnp.float32)
            values = jnp.concatenate([wide[kv_local:], wide[:kv_local]], axis=0)
            new_out[mine, layer] = jnp.dot(
                weights, values.astype(jnp.bfloat16), preferred_element_type=jnp.float32
            )
            new_peak[mine, layer] = jnp.broadcast_to(peak, (rows, head))
            new_sum[mine, layer] = jnp.broadcast_to(total, (rows, head))

    own_queries.wait()
    for copy in query_copies:
        copy.wait()
    for copy in own_pages:
        copy.wait()

    token_ids = lax.broadcasted_iota(jnp.int32, (1, page_len), 1)

    def attend(slot):
        query_rows = rows_of(layer_queries[at_slot(request_of, slot)])
        scores = scores_of(query_rows, pages[0][slot])
        for place in range(1, kv_local):
            scores = jnp.where(
                row_head == place, scores_of(query_rows, pages[place][slot]), scores
            )
        peak, weights, total = softmax_parts(scores, token_ids < at_slot(live, slot))
        out = jnp.dot(weights, pages[kv_local][slot], preferred_element_type=jnp.float32)
        for place in range(1, kv_local):
            out = jnp.where(
                row_head == place,
                jnp.dot(weights, pages[kv_local + place][slot], preferred_element_type=jnp.float32),
                out,
            )
        page_out[slot] = out
        page_peak[slot] = jnp.broadcast_to(peak, (rows, head))
        page_sum[slot] = jnp.broadcast_to(total, (rows, head))

    def page_for(key):
        slot, keep = 0, 0
        for q in range(positions):
            hit = (keys[q] == key).astype(jnp.int32)
            slot += hit * q
            keep += hit * used[q]
        return jnp.minimum(slot, positions - 1), keep

    key_copies = [[] for _ in chunks]

    def send(chunk):
        for key in sent_keys + (0,):
            slot, keep = page_for(key)
            page = pages[chunk][slot]
            page = lax.select(keep > 0, page, jnp.zeros_like(page))
            if key == 0:
                landing[chunk][0] = page
                continue
            leaving[key, chunk] = page
            copy = pltpu.make_async_remote_copy(
                src_ref=leaving.at[key, chunk],
                dst_ref=landing[chunk].at[key],
                send_sem=key_send.at[key, chunk],
                recv_sem=key_recv.at[key, chunk],
                device_id={"batch": exclusive_or(batch, key, batches)},
                device_id_type=MESH,
            )
            copy.start()
            key_copies[chunk].append(copy)

    for chunk, (entry, place) in enumerate(chunks):
        for copy in page_copies[chunk]:
            copy.wait_recv()
        if by_key:
            send(chunk)
        if chunk < local_pages:
            attend(tensor * local_pages + chunk)
    for page in range(len(chunks), local_pages):
        attend(tensor * local_pages + page)
    for page in range(local_pages):
        for ahead in range(1, tensors):
            attend(lax.rem(tensor + tensors - ahead, tensors) * local_pages + page)

    lane = lax.broadcasted_iota(jnp.int32, (rows, head), 1)

    def merge(request):
        takes = [
            (request_of[slot] == request) & (used[slot] > 0) for slot in range(positions)
        ]
        top = jnp.full((rows, head), MASKED, jnp.float32)
        for slot in range(positions):
            top = jnp.maximum(top, jnp.where(takes[slot], page_peak[slot], MASKED))
        numerator = jnp.zeros((rows, head), jnp.float32)
        denominator = jnp.zeros((rows, head), jnp.float32)
        for slot in range(positions):
            factor = jnp.where(takes[slot], jnp.exp(page_peak[slot] - top), 0.0)
            numerator += factor * page_out[slot]
            denominator += factor * page_sum[slot]
        return numerator, jnp.where(lane < head // 2, top, denominator)

    part_copies = []
    for ahead in range(1, sections):
        other = lax.rem(section + ahead, sections)
        for mine in range(owned):
            numerator, stats = merge(other * owned + mine)
            outgoing[ahead - 1, mine, 0] = numerator
            outgoing[ahead - 1, mine, 1] = stats
        copy = pltpu.make_async_remote_copy(
            src_ref=outgoing.at[ahead - 1],
            dst_ref=merged.at[section],
            send_sem=part_sems.at[0, ahead - 1],
            recv_sem=part_sems.at[1, ahead - 1],
            device_id={"section": other},
            device_id_type=MESH,
        )
        copy.start()
        part_copies.append(copy)
    for mine in range(owned):
        numerator, stats = merge(section * owned + mine)
        merged[section, mine, 0] = numerator
        merged[section, mine, 1] = stats

    if not by_key:
        for slot in range(positions):
            for chunk, (entry, place) in enumerate(chunks):
                page = pages[chunk][slot]
                slots_out[slot][entry, place] = lax.select(
                    used[slot] > 0, page, jnp.zeros_like(page)
                )

    for copy in part_copies:
        copy.wait()
    for mine in range(owned):
        for layer in range(layers):
            numerator, stats = merged[layer, mine, 0], merged[layer, mine, 1]
            top, denominator = stats[:, :1], stats[:, head // 2 : head // 2 + 1]
            latest = new_peak[mine, layer]
            joint = jnp.maximum(top, latest)
            old_scale, new_scale = jnp.exp(top - joint), jnp.exp(latest - joint)
            result = (old_scale * numerator + new_scale * new_out[mine, layer]) / (
                old_scale * denominator + new_scale * new_sum[mine, layer]
            )
            attended[mine, layer] = result.reshape(steps, heads, head).astype(jnp.bfloat16)
    for chunk, (entry, place) in enumerate(chunks):
        if by_key:
            for copy in key_copies[chunk]:
                copy.wait_recv()
            for slot in range(positions):
                slots_out[0][slot, entry, place] = landing[chunk][
                    jnp.minimum(keys[slot], batches - 1)
                ]
    for chunk in range(len(chunks)):
        for copy in page_copies[chunk] + key_copies[chunk]:
            copy.wait_send()


def attend_and_order(prefill_cache, lengths, page_table, holder, queries, new_kv, sent_keys, number):
    tensors, sections = lax.axis_size("tensor"), lax.axis_size("section")
    batches, positions = holder.shape
    local_pages, cache_heads, page_len, head = (
        prefill_cache.shape[1],
        prefill_cache.shape[3],
        prefill_cache.shape[4],
        prefill_cache.shape[5],
    )
    kv_local = cache_heads // tensors
    owned, layers, steps, heads = queries.shape[:4]
    rows = steps * heads
    new_rows = new_kv.reshape(owned, layers, steps * 2 * kv_local, head)
    page = jax.ShapeDtypeStruct((2, kv_local, page_len, head), jnp.bfloat16)
    smem = pl.BlockSpec(memory_space=pltpu.SMEM)
    vmem = pl.BlockSpec(memory_space=pltpu.VMEM)

    def wide(*lead):
        return pltpu.VMEM(lead + (rows, head), jnp.float32)

    if sent_keys is not None:
        outs = [jax.ShapeDtypeStruct((positions,) + page.shape, page.dtype)]
        key_scratch = [
            pltpu.VMEM((batches, 2 * kv_local, page_len, head), jnp.bfloat16),
            pltpu.SemaphoreType.DMA((batches, 2 * kv_local)),
            pltpu.SemaphoreType.DMA((batches, 2 * kv_local)),
            *[pltpu.VMEM((batches, page_len, head), jnp.bfloat16)] * (2 * kv_local),
        ]
    else:
        outs, key_scratch = [page] * positions, []
    result = pl.pallas_call(
        functools.partial(kernel, tensors, sections, batches, sent_keys),
        out_shape=outs + [jax.ShapeDtypeStruct(queries.shape, jnp.bfloat16)],
        in_specs=[smem, smem, smem, pl.BlockSpec(memory_space=pl.ANY), vmem, vmem],
        out_specs=[vmem] * (len(outs) + 1),
        scratch_shapes=[
            *[pltpu.VMEM((positions, page_len, head), jnp.bfloat16)] * (2 * kv_local),
            pltpu.VMEM((owned * sections, steps, heads, head), jnp.bfloat16),
            wide(positions), wide(positions), wide(positions),
            wide(owned, layers), wide(owned, layers), wide(owned, layers),
            wide(max(sections - 1, 1), owned, 2),
            wide(sections, owned, 2),
            pltpu.SemaphoreType.DMA((1 + 2 * kv_local,)),
            pltpu.SemaphoreType.DMA((max(tensors - 1, 1), local_pages, 2 * kv_local)),
            pltpu.SemaphoreType.DMA((max(tensors - 1, 1), local_pages, 2 * kv_local)),
            pltpu.SemaphoreType.DMA((2, max(sections - 1, 1))),
            pltpu.SemaphoreType.DMA((2, max(sections - 1, 1))),
        ] + key_scratch,
        compiler_params=pltpu.CompilerParams(collective_id=number, has_side_effects=True),
        name=f"attend_and_order_{number}",
    )(lengths, page_table.reshape(-1), holder[0], prefill_cache, queries, new_rows)
    return result[:-1], result[-1]


def on_device(prefill_cache, lengths, page_table, holder, queries, new_kv):
    batch_count, positions = holder.shape
    route_keys = holder[0]
    by_key = sends_by_key(batch_count, positions)
    arrays = (prefill_cache, lengths, page_table, holder, queries, new_kv)
    if by_key:
        half = batch_count // 2
        far = tuple(range(half, half + batch_count // 4))
        chosen = jnp.zeros((), jnp.int32)
        branches = []
        for place, key in enumerate(far):
            chosen += jnp.any(route_keys == key).astype(jnp.int32) * (1 << place)
        for number in range(1 << len(far)):
            left_out = [key for place, key in enumerate(far) if not number >> place & 1]
            sent = tuple(key for key in range(1, batch_count) if key not in left_out)
            branches.append(
                lambda *given, sent=sent, number=number: attend_and_order(*given, sent, number)
            )
        (decode_slots,), attended = lax.switch(chosen, branches, *arrays)
    else:
        pages, attended = attend_and_order(*arrays, None, 0)
        moving = (jnp.stack(pages),)
        for bit in range(lax.axis_size("batch").bit_length() - 1):
            take = route_keys // (1 << bit) % 2 == 1
            partner = jax.tree.map(
                lambda part, own: part.astype(own.dtype),
                partner_2(shortened(moving), "batch", bit),
                moving,
            )
            moving = pick_where(take, partner, moving)
        decode_slots = moving[0]
    return (attended, decode_slots.reshape((1,) + decode_slots.shape))


def solution(mesh):
    placed = (
        P("section", ("batch", "tensor"), None, None, None, None),
        P("batch"),
        P("batch", None),
        P(),
        P(("batch", "section"), None, None, "tensor", None),
        P(("batch", "section"), None, None, None, "tensor", None),
    )
    return jax.shard_map(
        on_device,
        mesh=mesh,
        in_specs=placed,
        out_specs=(
            P(("batch", "section"), None, None, "tensor", None),
            P("section", "batch", None, "tensor", None, None),
        ),
        check_vma=False,
    )
```
